512 devices in a mesh: ctx: 32 (over x, y), tp: 16 (over z, core).
Axes of the slice: x: 4, y: 8, z: 8, core: 2. Of those that a mesh axis runs over, the one named last changes fastest.
Arguments:
- queries: bfloat16 [16384, 8192], P('ctx', 'tp'), may hold values from -1.796875 to 1.796875
- keys: bfloat16 [16384, 8192], P('ctx', 'tp'), may hold values from -1.796875 to 1.796875
- values: bfloat16 [16384, 8192], P('ctx', 'tp'), may hold values from -12 to 12
- log_decay: float32 [64, 16384], P('tp', 'ctx'), may hold values from -2 to 0
- gain: float32 [8192], P('tp'), may hold values from 0.1 to 1.9
- grad_out: bfloat16 [16384, 8192], P('ctx', 'tp'), may hold values from -5 to 5
Outputs:
- normed: bfloat16 [16384, 8192], P('ctx', 'tp')
- grad_queries: bfloat16 [16384, 8192], P('ctx', 'tp')
- grad_keys: bfloat16 [16384, 8192], P('ctx', 'tp')
- grad_values: bfloat16 [16384, 8192], P('ctx', 'tp')
The draws below stay inside these ranges and needn't reach their ends.
All inputs are finite; a program needn't handle non-finite values.
Results may differ from the reference program's by a relative error of at most 0.0069.
Values sent between devices are 32-bit elements; how exact they have to be, the bound alone decides.
A program may use at most 64 MiB of HBM per device.

```python
import math
import jax
import jax.numpy as jnp
from jax import lax

ATTENTION_HEADS = 64
E = 128
BLOCK = 512
SEQUENCE_TOKENS = 16384


def head_rates(key):
    base = jax.random.fold_in(key, 11)
    picked = jax.random.randint(jax.random.fold_in(base, 1), (ATTENTION_HEADS,), 0, 100)
    share = 50
    fast_rate = jnp.exp(jax.random.uniform(jax.random.fold_in(base, 2), (ATTENTION_HEADS,), jnp.float32, math.log(1.0 / 50.0), math.log(1.0 / 30.0)))
    slow_rate = 0.5 * math.log(2.0) / SEQUENCE_TOKENS * jnp.exp(jax.random.uniform(jax.random.fold_in(base, 3), (ATTENTION_HEADS,), jnp.float32, math.log(0.5), 0.0))
    return jnp.where(picked < share, fast_rate, slow_rate)


def draw_log_decay(key, part):
    decay_rates = head_rates(key)
    local = jax.random.fold_in(key, 23)
    decay_factor = jnp.exp(jax.random.uniform(jax.random.fold_in(local, 1), (ATTENTION_HEADS, SEQUENCE_TOKENS), jnp.float32, math.log(0.5), math.log(2.0)))
    position_slots = jax.random.randint(jax.random.fold_in(local, 2), (ATTENTION_HEADS, 3), 0, SEQUENCE_TOKENS)
    retained_fraction = jax.random.uniform(jax.random.fold_in(local, 3), (ATTENTION_HEADS, 3), jnp.float32, 0.6, 0.8)
    token_positions = jnp.arange(SEQUENCE_TOKENS, dtype=jnp.int32)
    decay_windows = jnp.zeros((ATTENTION_HEADS, SEQUENCE_TOKENS), jnp.float32)
    for column_offset in range(3):
        decay_windows = decay_windows + jnp.where(token_positions[None, :] == position_slots[:, column_offset:column_offset + 1], jnp.log(retained_fraction[:, column_offset:column_offset + 1]), 0.0)
    return (-decay_rates[:, None] * decay_factor + decay_windows).astype(jnp.float32)


def draw_values(key, part):
    decay_rates = head_rates(key)
    rising = jnp.power(3.0, jnp.arange(ATTENTION_HEADS, dtype=jnp.float32) / (ATTENTION_HEADS - 1))
    scales = rising * jnp.sqrt(jnp.minimum(1.0, 40.0 * decay_rates))
    noise_key = jax.random.fold_in(key, 31)
    noise = jnp.clip(jax.random.normal(noise_key, (SEQUENCE_TOKENS, ATTENTION_HEADS, E), jnp.float32), -4.0, 4.0)
    return (noise * scales[None, :, None]).reshape(SEQUENCE_TOKENS, ATTENTION_HEADS * E).astype(jnp.bfloat16)


def level_of(rng, extent, shards, low, largest):
    loudness = 1.0
    for position, shards_of in shards:
        steps = jax.random.uniform(jax.random.fold_in(jax.random.fold_in(rng, 6), position), (shards_of,), jnp.float32, low / len(shards), largest / len(shards))
        loudness = loudness * jnp.repeat(jnp.exp(steps), extent[position] // shards_of).reshape((-1,) + (1,) * (len(extent) - 1 - position))
    return loudness


def gaussian(key, dims, deviation, bound, cuts=(), kind=jnp.bfloat16):
    entries = jax.random.normal(key, dims, jnp.float32) * deviation
    if len(cuts) > 0:
        entries = level_of(key, dims, cuts, -0.22, 0.18) * entries
    return jnp.clip(entries, min=-bound, max=bound).astype(kind)


def setup_inputs(seed: int = 0) -> dict:
    key_list = jax.random.split(jax.random.key(seed), 7)
    return {
        "queries": gaussian(key_list[0], (SEQUENCE_TOKENS, ATTENTION_HEADS * E), 0.3, 1.796875, ((0, 32), (1, 16))),
        "keys": gaussian(key_list[1], (SEQUENCE_TOKENS, ATTENTION_HEADS * E), 0.3, 1.796875, ((0, 32), (1, 16))),
        "values": draw_values(jax.random.fold_in(key_list[6], 71), 0),
        "log_decay": draw_log_decay(jax.random.fold_in(key_list[6], 71), 0),
        "gain": jnp.clip(1.0 + 0.18 * jax.random.normal(key_list[4], (ATTENTION_HEADS * E,), jnp.float32), 0.1, 1.9),
        "grad_out": gaussian(key_list[5], (SEQUENCE_TOKENS, ATTENTION_HEADS * E), 1.0, 5.0, ((0, 32), (1, 16))),
    }


def half(matrix):
    return lax.optimization_barrier(matrix.astype(jnp.bfloat16))

def wide(matrix):
    return matrix.astype(jnp.float32)

def prepare(query_blk, key_blk, decay_blk):
    cumulative = jnp.cumsum(decay_blk, axis=1)
    totals = cumulative[:, -1]
    row_pos = lax.broadcasted_iota(jnp.int32, (BLOCK, BLOCK), 0)
    col_pos = lax.broadcasted_iota(jnp.int32, (BLOCK, BLOCK), 1)
    causal = row_pos >= col_pos
    spread = cumulative[:, :, None] - cumulative[:, None, :]
    weights = jnp.exp(jnp.where(causal[None], spread, -1e+30))
    scores = jnp.einsum('the,she->hts', wide(query_blk), wide(key_blk))
    probs = half(scores * weights)
    rise = jnp.exp(cumulative).T[:, :, None]
    fall = jnp.exp(totals[:, None] - cumulative).T[:, :, None]
    query_dec = half(wide(query_blk) * rise)
    key_dec = half(wide(key_blk) * fall)
    return (weights, probs, rise, fall, query_dec, key_dec, jnp.exp(totals))

def reference(queries, keys, values, log_decay, gain, grad_out):
    blocks = SEQUENCE_TOKENS // BLOCK
    shape_four = (blocks, BLOCK, ATTENTION_HEADS, E)
    query_all = queries.reshape(shape_four)
    key_all = keys.reshape(shape_four)
    value_all = values.reshape(shape_four)
    decay_all = log_decay.reshape(ATTENTION_HEADS, blocks, BLOCK).transpose(1, 0, 2)

    def forward_step(state, pieces):
        query_blk, key_blk, value_blk, decay_blk = pieces
        weights, probs, rise, fall, query_dec, key_dec, decay_factor = prepare(query_blk, key_blk, decay_blk)
        state_half = half(state)
        attended = jnp.einsum('hts,she->the', wide(probs), wide(value_blk)) + jnp.einsum('the,hef->thf', wide(query_dec), wide(state_half))
        contrib = jnp.einsum('she,shf->hef', wide(key_dec), wide(value_blk))
        return (decay_factor[:, None, None] * state + contrib, (attended, state))
    start_state = jnp.zeros((ATTENTION_HEADS, E, E), jnp.float32)
    final_state, outputs = lax.scan(forward_step, start_state, (query_all, key_all, value_all, decay_all))
    attended, entering = outputs
    attended = attended.reshape(SEQUENCE_TOKENS, ATTENTION_HEADS * E)
    squares = lax.optimization_barrier(jnp.sum(attended * attended, axis=1))
    inverse = lax.rsqrt(squares / (ATTENTION_HEADS * E) + 1e-05)
    normed = (gain[None, :] * attended * inverse[:, None]).astype(jnp.bfloat16)
    scaled_grad = gain[None, :] * grad_out.astype(jnp.float32)
    crossed = lax.optimization_barrier(jnp.sum(scaled_grad * attended, axis=1))
    d_attended = (inverse[:, None] * scaled_grad - attended * (inverse ** 3 * crossed / (ATTENTION_HEADS * E))[:, None]).astype(jnp.bfloat16)
    grad_all = d_attended.reshape(shape_four)

    def backward_step(outflow, pieces):
        query_blk, key_blk, value_blk, decay_blk, grad_blk, state = pieces
        weights, probs, rise, fall, query_dec, key_dec, decay_factor = prepare(query_blk, key_blk, decay_blk)
        d_prob = jnp.einsum('the,she->hts', wide(grad_blk), wide(value_blk))
        d_scores = half(d_prob * weights)
        leave_half = half(outflow)
        state_half = half(state)
        grad_q = jnp.einsum('hts,she->the', wide(d_scores), wide(key_blk)) + rise * jnp.einsum('thf,hef->the', wide(grad_blk), wide(state_half))
        grad_k = jnp.einsum('hts,the->she', wide(d_scores), wide(query_blk)) + fall * jnp.einsum('shf,hef->she', wide(value_blk), wide(leave_half))
        grad_v = jnp.einsum('hts,the->she', wide(probs), wide(grad_blk)) + jnp.einsum('she,hef->shf', wide(key_dec), wide(leave_half))
        state_grad = jnp.einsum('the,thf->hef', wide(query_dec), wide(grad_blk))
        return (decay_factor[:, None, None] * outflow + state_grad, (grad_q, grad_k, grad_v))
    end_grad = jnp.zeros((ATTENTION_HEADS, E, E), jnp.float32)
    first_grad, grads = lax.scan(backward_step, end_grad, (query_all, key_all, value_all, decay_all, grad_all, entering), reverse=True)
    grad_q, grad_k, grad_v = grads
    return (normed, grad_q.reshape(SEQUENCE_TOKENS, ATTENTION_HEADS * E).astype(jnp.bfloat16), grad_k.reshape(SEQUENCE_TOKENS, ATTENTION_HEADS * E).astype(jnp.bfloat16), grad_v.reshape(SEQUENCE_TOKENS, ATTENTION_HEADS * E).astype(jnp.bfloat16))
```

```python
import jax
import jax.numpy as jnp
from jax import lax
from jax.experimental import pallas as pl
from jax.experimental.pallas import tpu as pltpu
from jax.sharding import PartitionSpec as P

ATTENTION_HEADS = 64
E = 128
BLOCK = 512
EPSILON = 1e-05

X, Y, TP = 4, 8, 16
HEADS = ATTENTION_HEADS // TP
PART = HEADS * E // Y
TILE = 128
F32, BF16 = jnp.float32, jnp.bfloat16

NN = (((1,), (0,)), ((), ()))
NT = (((1,), (1,)), ((), ()))
TN = (((0,), (0,)), ((), ()))


def dot(a, b, dims):
    return lax.dot_general(a, b, dims, preferred_element_type=F32)


def columns(row, width=TILE):
    return jnp.transpose(jnp.broadcast_to(row, (width, row.shape[1])))


def kernel(
    q_in, k_in, v_in, decay_in, gain_in, grad_in,
    normed_out, gq_out, gk_out, gv_out,
    q, k, v, decay, gain, grad,
    normed, gq, gk, gv,
    cum, col, rise, fall, qdec, kdec, weights, probs, dscores,
    att, squares, crosses, datt, half, gk_part, gv_part,
    factor_send, factor_recv, row_factor,
    part_f, recv_f, rows_f, back_f, state_f,
    part_b, recv_b, rows_b, back_b, state_b,
    stats,
    load_sem, store_sem,
    factor_ssem, factor_rsem, row_ssem, row_rsem,
    part_ssem, part_rsem, rows_ssem, rows_rsem, back_ssem, back_rsem,
    stat_ssem, stat_rsem,
):
    ctx, tp = lax.axis_index("ctx"), lax.axis_index("tp")
    x, y = ctx // Y, ctx % Y

    loads = [
        pltpu.make_async_copy(src, dst, load_sem.at[n])
        for n, (src, dst) in enumerate(
            ((decay_in, decay), (k_in, k), (v_in, v), (q_in, q), (gain_in, gain), (grad_in, grad))
        )
    ]
    for load in loads:
        load.start()

    def along_y(step):
        return (y + step) % Y

    def along_x(step):
        return (x + step) % X

    def along_tp(step):
        return (tp + step) % TP

    Y_STEPS = (4, 3, 5, 2, 6, 1, 7)
    X_STEPS = (2, 1, 3)
    TP_STEPS = (8, 9, 7, 10, 6, 11, 5, 12, 4, 13, 3, 14, 2, 15, 1)

    barrier = pltpu.get_barrier_semaphore()
    for step in Y_STEPS:
        pl.semaphore_signal(
            barrier, 1, device_id=(x * Y + along_y(step), tp), device_id_type=pl.DeviceIdType.MESH
        )
    for step in X_STEPS:
        pl.semaphore_signal(
            barrier, 1, device_id=(along_x(step) * Y + y, tp), device_id_type=pl.DeviceIdType.MESH
        )
    for step in TP_STEPS:
        pl.semaphore_signal(
            barrier, 1, device_id=(ctx, along_tp(step)), device_id_type=pl.DeviceIdType.MESH
        )

    def remote(src, dst, ssem, rsem, to_ctx, to_tp):
        return pltpu.make_async_remote_copy(
            src_ref=src, dst_ref=dst, send_sem=ssem, recv_sem=rsem,
            device_id=(to_ctx, to_tp), device_id_type=pl.DeviceIdType.MESH,
        )

    def spread_y(source, target, ssem, rsem):
        copies = []
        for step in Y_STEPS:
            to = along_y(step)
            copies.append(
                remote(source(to), target.at[y], ssem.at[to], rsem.at[y], x * Y + to, tp)
            )
            copies[-1].start()
        return copies

    def spread_x(source, target, ssem, rsem):
        copies = []
        for step in X_STEPS:
            to = along_x(step)
            copies.append(
                remote(source, target.at[x], ssem.at[to], rsem.at[x], to * Y + y, tp)
            )
            copies[-1].start()
        return copies

    def arrived_y(target, rsem, ssem):
        for step in Y_STEPS:
            at = along_y(step)
            remote(target.at[at], target.at[at], ssem.at[at], rsem.at[at], x * Y + at, tp).wait_recv()

    def arrived_x(target, rsem, ssem):
        for step in X_STEPS:
            at = along_x(step)
            remote(target.at[at], target.at[at], ssem.at[at], rsem.at[at], at * Y + y, tp).wait_recv()

    sent = []

    loads[0].wait()
    tokens = lax.broadcasted_iota(jnp.int32, (BLOCK, BLOCK), 0)
    until = lax.broadcasted_iota(jnp.int32, (BLOCK, BLOCK), 1)
    upper = jnp.where(tokens <= until, 1.0, 0.0).astype(F32)
    cum[...] = lax.dot_general(
        decay[...], upper, NN, precision=lax.Precision.HIGHEST, preferred_element_type=F32
    )
    for h in range(HEADS):
        row = cum[h : h + 1, :]
        total = row[:, BLOCK - 1 : BLOCK]
        factor_send[h] = jnp.exp(jnp.broadcast_to(total, (1, TILE)))
        wide = columns(row)
        col[h] = wide
        rise[h] = jnp.exp(wide)
        fall[h] = jnp.exp(total - wide)
    loads[1].wait()
    loads[2].wait()
    for h in range(HEADS):
        lanes = slice(h * E, (h + 1) * E)
        kdec[:, lanes] = (k[:, lanes].astype(F32) * fall[h]).astype(BF16)
        contrib = dot(kdec[:, lanes], v[:, lanes], TN)
        part_f[2 * h] = contrib[:PART]
        part_f[2 * h + 1] = contrib[PART:]

    pl.semaphore_wait(barrier, Y + X + TP - 3)
    sent += spread_y(lambda to: factor_send.at[to // 2], factor_recv, factor_ssem, factor_rsem)
    sent += spread_y(lambda to: part_f.at[to], recv_f, part_ssem.at[0], part_rsem.at[0])
    factor_recv[y] = factor_send[y // 2]
    recv_f[y] = part_f[y]

    loads[3].wait()

    def inside(h, carry):
        lanes = pl.ds(pl.multiple_of(h * E, E), E)
        qdec[:, lanes] = (q[:, lanes].astype(F32) * rise[h]).astype(BF16)
        row = cum[pl.ds(h, 1), :]
        for r in range(BLOCK // TILE):
            rows, width = slice(r * TILE, (r + 1) * TILE), (r + 1) * TILE
            scores = dot(q[rows, lanes], k[:width, lanes], NT)
            mine = col[h, rows, :]
            pieces = []
            for c in range(r + 1):
                spread = mine - row[:, c * TILE : (c + 1) * TILE]
                if c == r:
                    down = lax.broadcasted_iota(jnp.int32, (TILE, TILE), 0)
                    across = lax.broadcasted_iota(jnp.int32, (TILE, TILE), 1)
                    spread = jnp.where(down >= across, spread, -1e30)
                pieces.append(jnp.exp(spread))
            weight = pieces[0] if r == 0 else jnp.concatenate(pieces, axis=1)
            weights[h, rows, :width] = weight
            prob = (scores * weight).astype(BF16)
            probs[h, rows, :width] = prob
            att[rows, lanes] = dot(prob, v[:width, lanes], NN)
        return carry

    lax.fori_loop(0, HEADS, inside, 0)

    arrived_y(factor_recv, factor_rsem, factor_ssem)
    product = factor_recv[0]
    for j in range(1, Y):
        product = product * factor_recv[j]
    row_factor[x] = product
    sent += spread_x(row_factor.at[x], row_factor, row_ssem, row_rsem)

    def chain(order_y, order_x, before, recv, rows, back, state, n):
        running = recv[order_y[0]]
        back[order_y[0]] = jnp.zeros((PART, E), F32)
        for j in order_y[1:]:
            back[j] = running
            running = factor_recv[j] * running + recv[j]
        rows[x] = running
        copies = spread_x(rows.at[x], rows, rows_ssem.at[n], rows_rsem.at[n])
        if n == 0:
            arrived_x(row_factor, row_rsem, row_ssem)
        arrived_x(rows, rows_rsem.at[n], rows_ssem.at[n])
        enter = jnp.zeros((PART, E), F32)
        for i in order_x[:-1]:
            enter = jnp.where(before(i), row_factor[i] * enter + rows[i], enter)
        passed = enter
        for j in order_y:
            back[j] = back[j] + passed
            passed = factor_recv[j] * passed
        copies += spread_y(lambda to: back.at[to], state, back_ssem.at[n], back_rsem.at[n])
        state[y] = back[y]
        return copies

    arrived_y(recv_f, part_rsem.at[0], part_ssem.at[0])
    sent += chain(
        list(range(Y)), list(range(X)), lambda i: i < x, recv_f, rows_f, back_f, state_f, 0
    )
    loads[4].wait()
    loads[5].wait()
    arrived_y(state_f, back_rsem.at[0], back_ssem.at[0])

    def across(h, carry):
        lanes = pl.ds(pl.multiple_of(h * E, E), E)
        entering = state_f[pl.ds(2 * h, 2)].reshape(E, E).astype(BF16)
        half[h] = entering
        whole = att[:, lanes] + dot(qdec[:, lanes], entering, NN)
        att[:, lanes] = whole
        cotangent = gain[:, lanes] * grad[:, lanes].astype(F32)
        first = h == 0
        squares[...] = jnp.where(first, 0.0, squares[...]) + whole * whole
        crosses[...] = jnp.where(first, 0.0, crosses[...]) + cotangent * whole
        return carry

    squares[...] = jnp.zeros((BLOCK, E), F32)
    crosses[...] = jnp.zeros((BLOCK, E), F32)
    lax.fori_loop(0, HEADS, across, 0)

    own = jnp.concatenate(
        [
            jnp.sum(jnp.transpose(squares[...]), axis=0, keepdims=True),
            jnp.sum(jnp.transpose(crosses[...]), axis=0, keepdims=True),
        ],
        axis=0,
    )
    stats[tp] = own
    for step in TP_STEPS:
        to = along_tp(step)
        sent.append(
            remote(stats.at[tp], stats.at[tp], stat_ssem.at[to], stat_rsem.at[tp], ctx, to)
        )
        sent[-1].start()
    for step in TP_STEPS:
        at = along_tp(step)
        remote(stats.at[at], stats.at[at], stat_ssem.at[at], stat_rsem.at[at], ctx, at).wait_recv()
    sums = stats[0]
    for i in range(1, TP):
        sums = sums + stats[i]
    inverse_row = lax.rsqrt(sums[0:1] / (ATTENTION_HEADS * E) + EPSILON)
    slope_row = inverse_row * inverse_row * inverse_row * sums[1:2] / (ATTENTION_HEADS * E)
    squares[...] = columns(inverse_row)
    crosses[...] = columns(slope_row)

    def cotangents(h, carry):
        lanes = pl.ds(pl.multiple_of(h * E, E), E)
        inverse = squares[...]
        whole = att[:, lanes]
        scale = gain[:, lanes]
        here = (
            inverse * (scale * grad[:, lanes].astype(F32)) - whole * crosses[...]
        ).astype(BF16)
        datt[:, lanes] = here
        part_b[pl.ds(2 * h, 2)] = dot(qdec[:, lanes], here, TN).reshape(2, PART, E)
        return carry

    lax.fori_loop(0, HEADS, cotangents, 0)
    sent += spread_y(lambda to: part_b.at[to], recv_b, part_ssem.at[1], part_rsem.at[1])
    recv_b[y] = part_b[y]

    def backward(h, carry):
        lanes = pl.ds(pl.multiple_of(h * E, E), E)
        normed[:, lanes] = (gain[:, lanes] * att[:, lanes] * squares[...]).astype(BF16)
        entering = half[h]
        for r in range(BLOCK // TILE):
            rows, width = slice(r * TILE, (r + 1) * TILE), (r + 1) * TILE
            here = datt[rows, lanes]
            dprob = dot(here, v[:width, lanes], NT)
            dscore = (dprob * weights[h, rows, :width]).astype(BF16)
            dscores[h, rows, :width] = dscore
            gq[rows, lanes] = (
                dot(dscore, k[:width, lanes], NN) + rise[h, rows, :] * dot(here, entering, NT)
            ).astype(BF16)
        for c in range(BLOCK // TILE):
            place, later = slice(c * TILE, (c + 1) * TILE), slice(c * TILE, BLOCK)
            gk_part[place, lanes] = dot(dscores[h, later, place], q[later, lanes], TN)
            gv_part[place, lanes] = dot(probs[h, later, place], datt[later, lanes], TN)
        return carry

    lax.fori_loop(0, HEADS, backward, 0)
    stores = [
        pltpu.make_async_copy(src, dst, store_sem.at[n])
        for n, (src, dst) in enumerate(
            ((normed, normed_out), (gq, gq_out), (gk, gk_out), (gv, gv_out))
        )
    ]
    stores[0].start()
    stores[1].start()

    arrived_y(recv_b, part_rsem.at[1], part_ssem.at[1])
    sent += chain(
        list(reversed(range(Y))), list(reversed(range(X))), lambda i: i > x,
        recv_b, rows_b, back_b, state_b, 1,
    )
    arrived_y(state_b, back_rsem.at[1], back_ssem.at[1])

    def finish(h, carry):
        lanes = pl.ds(pl.multiple_of(h * E, E), E)
        leaving = state_b[pl.ds(2 * h, 2)].reshape(E, E).astype(BF16)
        gk[:, lanes] = (
            gk_part[:, lanes] + fall[h] * dot(v[:, lanes], leaving, NT)
        ).astype(BF16)
        gv[:, lanes] = (gv_part[:, lanes] + dot(kdec[:, lanes], leaving, NN)).astype(BF16)
        return carry

    lax.fori_loop(0, HEADS, finish, 0)
    stores[2].start()
    stores[3].start()
    for copy in sent:
        copy.wait_send()
    for store in stores:
        store.wait()


def per_device(queries, keys, values, log_decay, gain, grad_out):
    tile = jax.ShapeDtypeStruct((BLOCK, HEADS * E), BF16)
    flat16 = pltpu.VMEM((BLOCK, HEADS * E), BF16)
    flat32 = pltpu.VMEM((BLOCK, HEADS * E), F32)
    head32 = pltpu.VMEM((HEADS, BLOCK, E), F32)
    one32 = pltpu.VMEM((BLOCK, E), F32)
    square = (HEADS, BLOCK, BLOCK)
    parts = pltpu.VMEM((Y, PART, E), F32)
    across = pltpu.VMEM((X, PART, E), F32)
    sem = pltpu.SemaphoreType.DMA
    chain = [parts, parts, across, parts, parts]
    anywhere = pl.BlockSpec(memory_space=pl.ANY)
    return pl.pallas_call(
        kernel,
        out_shape=(tile,) * 4,
        in_specs=[anywhere] * 6,
        out_specs=(anywhere,) * 4,
        scratch_shapes=[
            flat16, flat16, flat16,
            pltpu.VMEM((HEADS, BLOCK), F32), pltpu.VMEM((1, HEADS * E), F32), flat16,
            flat16, flat16, flat16, flat16,
            pltpu.VMEM((HEADS, BLOCK), F32), head32, head32, head32, flat16, flat16,
            pltpu.VMEM(square, F32), pltpu.VMEM(square, BF16), pltpu.VMEM(square, BF16),
            flat32, one32, one32, flat16, pltpu.VMEM((HEADS, E, E), BF16), flat32, flat32,
            pltpu.VMEM((HEADS, 1, TILE), F32), pltpu.VMEM((Y, 1, TILE), F32),
            pltpu.VMEM((X, 1, TILE), F32),
            *chain, *chain,
            pltpu.VMEM((TP, 2, BLOCK), F32),
            sem((6,)), sem((4,)),
            sem((Y,)), sem((Y,)), sem((X,)), sem((X,)),
            sem((2, Y)), sem((2, Y)), sem((2, X)), sem((2, X)), sem((2, Y)), sem((2, Y)),
            sem((TP,)), sem((TP,)),
        ],
        compiler_params=pltpu.CompilerParams(collective_id=0, has_side_effects=True),
        name="layer",
    )(queries, keys, values, log_decay, gain.reshape(1, -1), grad_out)


def solution(mesh):
    in_specs = (
        P("ctx", "tp"),
        P("ctx", "tp"),
        P("ctx", "tp"),
        P("tp", "ctx"),
        P("tp"),
        P("ctx", "tp"),
    )
    out_specs = (P("ctx", "tp"), P("ctx", "tp"), P("ctx", "tp"), P("ctx", "tp"))
    return jax.shard_map(
        per_device, mesh=mesh, in_specs=in_specs, out_specs=out_specs, check_vma=False
    )
```

```python
import jax
import jax.numpy as jnp
from jax import lax
from jax.experimental import pallas as pl
from jax.experimental.pallas import tpu as pltpu
from jax.sharding import PartitionSpec as P

ATTENTION_HEADS = 64
E = 128
BLOCK = 512
EPSILON = 1e-05

X, Y, TP = 4, 8, 16
HEADS = ATTENTION_HEADS // TP
PART = E // Y
LAG = 2
TILE = 128
F32, BF16 = jnp.float32, jnp.bfloat16

NN = (((1,), (0,)), ((), ()))
NT = (((1,), (1,)), ((), ()))
TN = (((0,), (0,)), ((), ()))


def dot(a, b, dims):
    return lax.dot_general(a, b, dims, preferred_element_type=F32)


def columns(row, width=TILE):
    return jnp.transpose(jnp.broadcast_to(row, (width, row.shape[1])))


def kernel(
    q_in, k_in, v_in, decay_in, gain_in, grad_in,
    normed, gq, gk, gv,
    q, k, v, decay, gain, grad,
    cum, col, rise, fall, qdec, kdec, weights, probs, dscores,
    att, squares, crosses, datt, half, gk_part, gv_part,
    factor_send, factor_recv, row_factor,
    part_f, recv_f, rows_f, back_f, state_f,
    part_b, recv_b, rows_b, back_b, state_b,
    stats,
    load_sem,
    factor_ssem, factor_rsem, row_ssem, row_rsem,
    part_ssem, part_rsem, rows_ssem, rows_rsem, back_ssem, back_rsem,
    stat_ssem, stat_rsem,
):
    ctx, tp = lax.axis_index("ctx"), lax.axis_index("tp")
    x, y = ctx // Y, ctx % Y

    loads = [
        pltpu.make_async_copy(src, dst, load_sem.at[n])
        for n, (src, dst) in enumerate(
            ((decay_in, decay), (k_in, k), (v_in, v), (q_in, q), (gain_in, gain), (grad_in, grad))
        )
    ]
    for load in loads:
        load.start()

    def along_y(step):
        return (y + step) % Y

    def along_x(step):
        return (x + step) % X

    def along_tp(step):
        return (tp + step) % TP

    Y_STEPS = (4, 3, 5, 2, 6, 1, 7)
    X_STEPS = (2, 1, 3)
    TP_STEPS = (8, 9, 7, 10, 6, 11, 5, 12, 4, 13, 3, 14, 2, 15, 1)

    barrier = pltpu.get_barrier_semaphore()
    for step in Y_STEPS:
        pl.semaphore_signal(
            barrier, 1, device_id=(x * Y + along_y(step), tp), device_id_type=pl.DeviceIdType.MESH
        )
    for step in X_STEPS:
        pl.semaphore_signal(
            barrier, 1, device_id=(along_x(step) * Y + y, tp), device_id_type=pl.DeviceIdType.MESH
        )
    for step in TP_STEPS:
        pl.semaphore_signal(
            barrier, 1, device_id=(ctx, along_tp(step)), device_id_type=pl.DeviceIdType.MESH
        )

    def remote(src, dst, ssem, rsem, to_ctx, to_tp):
        return pltpu.make_async_remote_copy(
            src_ref=src, dst_ref=dst, send_sem=ssem, recv_sem=rsem,
            device_id=(to_ctx, to_tp), device_id_type=pl.DeviceIdType.MESH,
        )

    def spread_y(source, target, ssem, rsem):
        copies = []
        for step in Y_STEPS:
            to = along_y(step)
            copies.append(
                remote(source(to), target.at[y], ssem.at[to], rsem.at[y], x * Y + to, tp)
            )
            copies[-1].start()
        return copies

    def spread_x(source, target, ssem, rsem):
        copies = []
        for step in X_STEPS:
            to = along_x(step)
            copies.append(
                remote(source, target.at[x], ssem.at[to], rsem.at[x], to * Y + y, tp)
            )
            copies[-1].start()
        return copies

    def arrived_y(target, rsem, ssem):
        for step in Y_STEPS:
            at = along_y(step)
            remote(target.at[at], target.at[at], ssem.at[at], rsem.at[at], x * Y + at, tp).wait_recv()

    def arrived_x(target, rsem, ssem):
        for step in X_STEPS:
            at = along_x(step)
            remote(target.at[at], target.at[at], ssem.at[at], rsem.at[at], at * Y + y, tp).wait_recv()

    first, second, third, fourth = [], [], [], []

    loads[0].wait()
    tokens = lax.broadcasted_iota(jnp.int32, (BLOCK, BLOCK), 0)
    until = lax.broadcasted_iota(jnp.int32, (BLOCK, BLOCK), 1)
    upper = jnp.where(tokens <= until, 1.0, 0.0).astype(F32)
    cum[...] = lax.dot_general(
        decay[...], upper, NN, precision=lax.Precision.HIGHEST, preferred_element_type=F32
    )
    for h in range(HEADS):
        row = cum[h : h + 1, :]
        total = row[:, BLOCK - 1 : BLOCK]
        factor_send[h] = jnp.exp(jnp.broadcast_to(total, (1, TILE)))
        wide = columns(row)
        col[h] = wide
        rise[h] = jnp.exp(wide)
        fall[h] = jnp.exp(total - wide)
    loads[1].wait()
    loads[2].wait()
    for h in range(HEADS):
        lanes = slice(h * E, (h + 1) * E)
        kdec[:, lanes] = (k[:, lanes].astype(F32) * fall[h]).astype(BF16)
        part_f[h] = dot(kdec[:, lanes], v[:, lanes], TN).reshape(Y, PART, E)
        if h == 0:
            pl.semaphore_wait(barrier, Y + X + TP - 3)
            first += spread_y(lambda to: factor_send, factor_recv, factor_ssem, factor_rsem)
            factor_recv[y] = factor_send[...]
        first += spread_y(
            lambda to: part_f.at[h, to], recv_f.at[h], part_ssem.at[0, h], part_rsem.at[0, h]
        )
        recv_f[h, y] = part_f[h, y]

    loads[3].wait()

    def inside(h, carry):
        lanes = pl.ds(pl.multiple_of(h * E, E), E)
        qdec[:, lanes] = (q[:, lanes].astype(F32) * rise[h]).astype(BF16)
        row = cum[pl.ds(h, 1), :]
        for r in range(BLOCK // TILE):
            rows, width = slice(r * TILE, (r + 1) * TILE), (r + 1) * TILE
            scores = dot(q[rows, lanes], k[:width, lanes], NT)
            mine = col[h, rows, :]
            pieces = []
            for c in range(r + 1):
                spread = mine - row[:, c * TILE : (c + 1) * TILE]
                if c == r:
                    down = lax.broadcasted_iota(jnp.int32, (TILE, TILE), 0)
                    across = lax.broadcasted_iota(jnp.int32, (TILE, TILE), 1)
                    spread = jnp.where(down >= across, spread, -1e30)
                pieces.append(jnp.exp(spread))
            weight = pieces[0] if r == 0 else jnp.concatenate(pieces, axis=1)
            weights[h, rows, :width] = weight
            prob = (scores * weight).astype(BF16)
            probs[h, rows, :width] = prob
            att[rows, lanes] = dot(prob, v[:width, lanes], NN)
        return carry

    lax.fori_loop(0, HEADS, inside, 0)

    arrived_y(factor_recv, factor_rsem, factor_ssem)
    product = factor_recv[0]
    for j in range(1, Y):
        product = product * factor_recv[j]
    row_factor[x] = product
    first += spread_x(row_factor.at[x], row_factor, row_ssem, row_rsem)

    def chain(order_y, order_x, before, recv, rows, back, state, n):
        to_rows, to_places = [], []
        for turn in range(HEADS + LAG):
            h = turn
            if h < HEADS:
                arrived_y(recv.at[h], part_rsem.at[n, h], part_ssem.at[n, h])
                running = recv[h, order_y[0]]
                back[h, order_y[0]] = jnp.zeros((PART, E), F32)
                for j in order_y[1:]:
                    back[h, j] = running
                    running = factor_recv[j, h] * running + recv[h, j]
                rows[h, x] = running
                to_rows += spread_x(
                    rows.at[h, x], rows.at[h], rows_ssem.at[n, h], rows_rsem.at[n, h]
                )
            if n == 0 and turn == LAG:
                arrived_x(row_factor, row_rsem, row_ssem)
            h = turn - LAG
            if h >= 0:
                arrived_x(rows.at[h], rows_rsem.at[n, h], rows_ssem.at[n, h])
                enter = jnp.zeros((PART, E), F32)
                for i in order_x[:-1]:
                    enter = jnp.where(before(i), row_factor[i, h] * enter + rows[h, i], enter)
                for j in order_y:
                    back[h, j] = back[h, j] + enter
                    enter = factor_recv[j, h] * enter
                to_places += spread_y(
                    lambda to: back.at[h, to], state.at[h], back_ssem.at[n, h], back_rsem.at[n, h]
                )
                state[h, y] = back[h, y]
        return to_rows, to_places

    to_rows, to_places = chain(
        list(range(Y)), list(range(X)), lambda i: i < x, recv_f, rows_f, back_f, state_f, 0
    )
    first += to_rows
    second += to_places
    loads[4].wait()
    loads[5].wait()
    for copy in first:
        copy.wait_send()

    for h in range(HEADS):
        lanes = slice(h * E, (h + 1) * E)
        arrived_y(state_f.at[h], back_rsem.at[0, h], back_ssem.at[0, h])
        entering = state_f[h].reshape(E, E).astype(BF16)
        half[h] = entering
        whole = att[:, lanes] + dot(qdec[:, lanes], entering, NN)
        att[:, lanes] = whole
        cotangent = gain[:, lanes] * grad[:, lanes].astype(F32)
        square, cross = whole * whole, cotangent * whole
        squares[...] = square if h == 0 else squares[...] + square
        crosses[...] = cross if h == 0 else crosses[...] + cross

    own = jnp.concatenate(
        [
            jnp.sum(jnp.transpose(squares[...]), axis=0, keepdims=True),
            jnp.sum(jnp.transpose(crosses[...]), axis=0, keepdims=True),
        ],
        axis=0,
    )
    stats[tp] = own
    for step in TP_STEPS:
        to = along_tp(step)
        second.append(
            remote(stats.at[tp], stats.at[tp], stat_ssem.at[to], stat_rsem.at[tp], ctx, to)
        )
        second[-1].start()
    for step in TP_STEPS:
        at = along_tp(step)
        remote(stats.at[at], stats.at[at], stat_ssem.at[at], stat_rsem.at[at], ctx, at).wait_recv()
    sums = stats[0]
    for i in range(1, TP):
        sums = sums + stats[i]
    inverse_row = lax.rsqrt(sums[0:1] / (ATTENTION_HEADS * E) + EPSILON)
    slope_row = inverse_row * inverse_row * inverse_row * sums[1:2] / (ATTENTION_HEADS * E)
    squares[...] = columns(inverse_row)
    crosses[...] = columns(slope_row)

    for h in range(HEADS):
        lanes = slice(h * E, (h + 1) * E)
        inverse = squares[...]
        whole = att[:, lanes]
        scale = gain[:, lanes]
        here = (
            inverse * (scale * grad[:, lanes].astype(F32)) - whole * crosses[...]
        ).astype(BF16)
        datt[:, lanes] = here
        part_b[h] = dot(qdec[:, lanes], here, TN).reshape(Y, PART, E)
        third += spread_y(
            lambda to: part_b.at[h, to], recv_b.at[h], part_ssem.at[1, h], part_rsem.at[1, h]
        )
        recv_b[h, y] = part_b[h, y]

    def backward(h, carry):
        lanes = pl.ds(pl.multiple_of(h * E, E), E)
        normed[:, lanes] = (gain[:, lanes] * att[:, lanes] * squares[...]).astype(BF16)
        entering = half[h]
        for r in range(BLOCK // TILE):
            rows, width = slice(r * TILE, (r + 1) * TILE), (r + 1) * TILE
            here = datt[rows, lanes]
            dprob = dot(here, v[:width, lanes], NT)
            dscore = (dprob * weights[h, rows, :width]).astype(BF16)
            dscores[h, rows, :width] = dscore
            gq[rows, lanes] = (
                dot(dscore, k[:width, lanes], NN) + rise[h, rows, :] * dot(here, entering, NT)
            ).astype(BF16)
        for c in range(BLOCK // TILE):
            place, later = slice(c * TILE, (c + 1) * TILE), slice(c * TILE, BLOCK)
            gk_part[place, lanes] = dot(dscores[h, later, place], q[later, lanes], TN)
            gv_part[place, lanes] = dot(probs[h, later, place], datt[later, lanes], TN)
        return carry

    lax.fori_loop(0, HEADS, backward, 0)
    for copy in second:
        copy.wait_send()

    to_rows, to_places = chain(
        list(reversed(range(Y))), list(reversed(range(X))), lambda i: i > x,
        recv_b, rows_b, back_b, state_b, 1,
    )
    third += to_rows
    fourth += to_places
    for copy in third:
        copy.wait_send()
    for h in range(HEADS):
        lanes = slice(h * E, (h + 1) * E)
        if h == HEADS - 1:
            for copy in fourth:
                copy.wait_send()
        arrived_y(state_b.at[h], back_rsem.at[1, h], back_ssem.at[1, h])
        leaving = state_b[h].reshape(E, E).astype(BF16)
        gk[:, lanes] = (
            gk_part[:, lanes] + fall[h] * dot(v[:, lanes], leaving, NT)
        ).astype(BF16)
        gv[:, lanes] = (gv_part[:, lanes] + dot(kdec[:, lanes], leaving, NN)).astype(BF16)


def write(*refs):
    sources, results, sem = refs[:4], refs[4:8], refs[8]
    stores = [
        pltpu.make_async_copy(src, dst, sem.at[n])
        for n, (src, dst) in enumerate(zip(sources, results))
    ]
    for store in stores:
        store.start()
    for store in stores:
        store.wait()


def per_device(queries, keys, values, log_decay, gain, grad_out):
    tile = jax.ShapeDtypeStruct((BLOCK, HEADS * E), BF16)
    flat16 = pltpu.VMEM((BLOCK, HEADS * E), BF16)
    flat32 = pltpu.VMEM((BLOCK, HEADS * E), F32)
    head32 = pltpu.VMEM((HEADS, BLOCK, E), F32)
    one32 = pltpu.VMEM((BLOCK, E), F32)
    square = (HEADS, BLOCK, BLOCK)
    parts = pltpu.VMEM((HEADS, Y, PART, E), F32)
    across = pltpu.VMEM((HEADS, X, PART, E), F32)
    sem = pltpu.SemaphoreType.DMA
    chain = [parts, parts, across, parts, parts]
    anywhere = pl.BlockSpec(memory_space=pl.ANY)
    vmem = pl.BlockSpec(memory_space=pltpu.VMEM)
    results = pl.pallas_call(
        kernel,
        out_shape=(pltpu.VMEM((BLOCK, HEADS * E), BF16),) * 4,
        in_specs=[anywhere] * 6,
        out_specs=(vmem,) * 4,
        scratch_shapes=[
            flat16, flat16, flat16,
            pltpu.VMEM((HEADS, BLOCK), F32), pltpu.VMEM((1, HEADS * E), F32), flat16,
            pltpu.VMEM((HEADS, BLOCK), F32), head32, head32, head32, flat16, flat16,
            pltpu.VMEM(square, F32), pltpu.VMEM(square, BF16), pltpu.VMEM(square, BF16),
            flat32, one32, one32, flat16, pltpu.VMEM((HEADS, E, E), BF16), flat32, flat32,
            pltpu.VMEM((HEADS, 1, TILE), F32), pltpu.VMEM((Y, HEADS, 1, TILE), F32),
            pltpu.VMEM((X, HEADS, 1, TILE), F32),
            *chain, *chain,
            pltpu.VMEM((TP, 2, BLOCK), F32),
            sem((6,)),
            sem((Y,)), sem((Y,)), sem((X,)), sem((X,)),
            *[sem((2, HEADS, n)) for n in (Y, Y, X, X, Y, Y)],
            sem((TP,)), sem((TP,)),
        ],
        compiler_params=pltpu.CompilerParams(
            collective_id=0,
            has_side_effects=True,
            vmem_limit_bytes=67043328 - 4 * BLOCK * HEADS * E * 2,
        ),
        name="layer",
    )(queries, keys, values, log_decay, gain.reshape(1, -1), grad_out)
    return pl.pallas_call(
        write,
        out_shape=(tile,) * 4,
        in_specs=[vmem] * 4,
        out_specs=(anywhere,) * 4,
        scratch_shapes=[sem((4,))],
        compiler_params=pltpu.CompilerParams(vmem_limit_bytes=16 * 2**20),
        name="write",
    )(*results)


def solution(mesh):
    in_specs = (
        P("ctx", "tp"),
        P("ctx", "tp"),
        P("ctx", "tp"),
        P("tp", "ctx"),
        P("tp"),
        P("ctx", "tp"),
    )
    out_specs = (P("ctx", "tp"), P("ctx", "tp"), P("ctx", "tp"), P("ctx", "tp"))
    return jax.shard_map(
        per_device, mesh=mesh, in_specs=in_specs, out_specs=out_specs, check_vma=False
    )
```

```python
import jax
import jax.numpy as jnp
from jax import lax
from jax.experimental import pallas as pl
from jax.experimental.pallas import tpu as pltpu
from jax.sharding import PartitionSpec as P

ATTENTION_HEADS = 64
E = 128
BLOCK = 512
EPSILON = 1e-05

X, Y, Z, TP = 4, 8, 8, 16
HEADS = ATTENTION_HEADS // TP
PART = E // Y
GROUP = 2
CHUNKS = HEADS // GROUP
LAG = 1
TILE = 128
F32, BF16 = jnp.float32, jnp.bfloat16

NN = (((1,), (0,)), ((), ()))
NT = (((1,), (1,)), ((), ()))
TN = (((0,), (0,)), ((), ()))


def dot(a, b, dims):
    return lax.dot_general(a, b, dims, preferred_element_type=F32)


def columns(row, width=TILE):
    return jnp.transpose(jnp.broadcast_to(row, (width, row.shape[1])))


def kernel(
    q_in, k_in, v_in, decay_in, gain_in, grad_in,
    normed, gq, gk, gv,
    q, k, v, decay, gain, grad,
    cum, col, rise, fall, qdec, kdec, weights, probs, dscores,
    att, squares, crosses, datt, half, gk_part, gv_part,
    factor_send, factor_recv, row_factor,
    part_f, recv_f, rows_f, back_f, state_f,
    part_b, recv_b, rows_b, back_b, state_b,
    pair, stats,
    load_sem,
    factor_ssem, factor_rsem, row_ssem, row_rsem,
    part_ssem, part_rsem, rows_ssem, rows_rsem, back_ssem, back_rsem,
    pair_sem, stat_ssem, stat_rsem,
):
    ctx, tp = lax.axis_index("ctx"), lax.axis_index("tp")
    x, y = ctx // Y, ctx % Y
    z, core = tp // 2, tp % 2
    other = z * 2 + 1 - core

    loads = [
        pltpu.make_async_copy(src, dst, load_sem.at[n])
        for n, (src, dst) in enumerate(
            ((decay_in, decay), (k_in, k), (v_in, v), (q_in, q), (gain_in, gain), (grad_in, grad))
        )
    ]
    for load in loads:
        load.start()

    def along_y(step):
        return (y + step) % Y

    def along_x(step):
        return (x + step) % X

    def along_z(step):
        return (z + step) % Z

    Y_STEPS = (4, 3, 5, 2, 6, 1, 7)
    X_STEPS = (2, 1, 3)
    Z_STEPS = (4, 3, 5, 2, 6, 1, 7)

    barrier = pltpu.get_barrier_semaphore()
    for step in Y_STEPS:
        pl.semaphore_signal(
            barrier, 1, device_id=(x * Y + along_y(step), tp), device_id_type=pl.DeviceIdType.MESH
        )
    for step in X_STEPS:
        pl.semaphore_signal(
            barrier, 1, device_id=(along_x(step) * Y + y, tp), device_id_type=pl.DeviceIdType.MESH
        )
    for step in Z_STEPS:
        pl.semaphore_signal(
            barrier, 1, device_id=(ctx, along_z(step) * 2 + core), device_id_type=pl.DeviceIdType.MESH
        )
    pl.semaphore_signal(barrier, 1, device_id=(ctx, other), device_id_type=pl.DeviceIdType.MESH)

    def remote(src, dst, ssem, rsem, to_ctx, to_tp):
        return pltpu.make_async_remote_copy(
            src_ref=src, dst_ref=dst, send_sem=ssem, recv_sem=rsem,
            device_id=(to_ctx, to_tp), device_id_type=pl.DeviceIdType.MESH,
        )

    def spread_y(source, target, ssem, rsem):
        copies = []
        for step in Y_STEPS:
            to = along_y(step)
            copies.append(
                remote(source(to), target.at[y], ssem.at[to], rsem.at[y], x * Y + to, tp)
            )
            copies[-1].start()
        return copies

    def spread_x(source, target, ssem, rsem):
        copies = []
        for step in X_STEPS:
            to = along_x(step)
            copies.append(
                remote(source, target.at[x], ssem.at[to], rsem.at[x], to * Y + y, tp)
            )
            copies[-1].start()
        return copies

    def arrived_y(target, rsem, ssem):
        for step in Y_STEPS:
            at = along_y(step)
            remote(target.at[at], target.at[at], ssem.at[at], rsem.at[at], x * Y + at, tp).wait_recv()

    def arrived_x(target, rsem, ssem):
        for step in X_STEPS:
            at = along_x(step)
            remote(target.at[at], target.at[at], ssem.at[at], rsem.at[at], at * Y + y, tp).wait_recv()

    first, second, third, fourth = [], [], [], []

    loads[0].wait()
    tokens = lax.broadcasted_iota(jnp.int32, (TILE, TILE), 0)
    until = lax.broadcasted_iota(jnp.int32, (TILE, TILE), 1)
    upper = jnp.where(tokens <= until, 1.0, 0.0).astype(F32)
    before = jnp.zeros((HEADS, 1), F32)
    for c in range(BLOCK // TILE):
        place = slice(c * TILE, (c + 1) * TILE)
        summed = before + lax.dot_general(
            decay[:, place], upper, NN, precision=lax.Precision.HIGHEST,
            preferred_element_type=F32,
        )
        cum[:, place] = summed
        before = summed[:, TILE - 1 : TILE]
    for h in range(HEADS):
        row = cum[h : h + 1, :]
        total = row[:, BLOCK - 1 : BLOCK]
        factor_send[h] = jnp.exp(jnp.broadcast_to(total, (1, TILE)))
        wide = columns(row)
        col[h] = wide
        rise[h] = jnp.exp(wide)
        fall[h] = jnp.exp(total - wide)
    loads[1].wait()
    loads[2].wait()
    for h in range(HEADS):
        lanes = slice(h * E, (h + 1) * E)
        kdec[:, lanes] = (k[:, lanes].astype(F32) * fall[h]).astype(BF16)
        g, inner = h // GROUP, slice(h % GROUP * PART, (h % GROUP + 1) * PART)
        part_f[g, :, inner] = dot(kdec[:, lanes], v[:, lanes], TN).reshape(Y, PART, E)
        if h == 0:
            pl.semaphore_wait(barrier, Y + X + Z - 2)
            first += spread_y(lambda to: factor_send, factor_recv, factor_ssem, factor_rsem)
            factor_recv[y] = factor_send[...]
        if h % GROUP == GROUP - 1:
            first += spread_y(
                lambda to: part_f.at[g, to], recv_f.at[g], part_ssem.at[0, g], part_rsem.at[0, g]
            )
            recv_f[g, y] = part_f[g, y]

    loads[3].wait()

    def inside(h, carry):
        lanes = pl.ds(pl.multiple_of(h * E, E), E)
        qdec[:, lanes] = (q[:, lanes].astype(F32) * rise[h]).astype(BF16)
        row = cum[pl.ds(h, 1), :]
        for r in range(BLOCK // TILE):
            rows, width = slice(r * TILE, (r + 1) * TILE), (r + 1) * TILE
            scores = dot(q[rows, lanes], k[:width, lanes], NT)
            mine = col[h, rows, :]
            pieces = []
            for c in range(r + 1):
                spread = mine - row[:, c * TILE : (c + 1) * TILE]
                if c == r:
                    down = lax.broadcasted_iota(jnp.int32, (TILE, TILE), 0)
                    across = lax.broadcasted_iota(jnp.int32, (TILE, TILE), 1)
                    spread = jnp.where(down >= across, spread, -1e30)
                pieces.append(jnp.exp(spread))
            weight = pieces[0] if r == 0 else jnp.concatenate(pieces, axis=1)
            weights[h, rows, :width] = weight
            prob = (scores * weight).astype(BF16)
            probs[h, rows, :width] = prob
            att[rows, lanes] = dot(prob, v[:width, lanes], NN)
        return carry

    lax.fori_loop(0, HEADS, inside, 0)

    arrived_y(factor_recv, factor_rsem, factor_ssem)
    product = factor_recv[0]
    for j in range(1, Y):
        product = product * factor_recv[j]
    row_factor[x] = product
    first += spread_x(row_factor.at[x], row_factor, row_ssem, row_rsem)

    def chain(order_y, order_x, before, recv, rows, back, state, n):
        to_rows, to_places = [], []
        inners = [slice(i * PART, (i + 1) * PART) for i in range(GROUP)]
        for turn in range(CHUNKS + LAG):
            g = turn
            if g < CHUNKS:
                arrived_y(recv.at[g], part_rsem.at[n, g], part_ssem.at[n, g])
                for i, inner in enumerate(inners):
                    h = g * GROUP + i
                    running = recv[g, order_y[0], inner]
                    back[g, order_y[0], inner] = jnp.zeros((PART, E), F32)
                    for j in order_y[1:]:
                        back[g, j, inner] = running
                        running = factor_recv[j, h] * running + recv[g, j, inner]
                    rows[g, x, inner] = running
                to_rows += spread_x(
                    rows.at[g, x], rows.at[g], rows_ssem.at[n, g], rows_rsem.at[n, g]
                )
            if n == 0 and turn == LAG:
                arrived_x(row_factor, row_rsem, row_ssem)
            g = turn - LAG
            if g >= 0:
                arrived_x(rows.at[g], rows_rsem.at[n, g], rows_ssem.at[n, g])
                for i, inner in enumerate(inners):
                    h = g * GROUP + i
                    enter = jnp.zeros((PART, E), F32)
                    for k in order_x[:-1]:
                        enter = jnp.where(
                            before(k), row_factor[k, h] * enter + rows[g, k, inner], enter
                        )
                    for j in order_y:
                        back[g, j, inner] = back[g, j, inner] + enter
                        enter = factor_recv[j, h] * enter
                to_places += spread_y(
                    lambda to: back.at[g, to], state.at[g], back_ssem.at[n, g], back_rsem.at[n, g]
                )
                state[g, y] = back[g, y]
        return to_rows, to_places

    to_rows, to_places = chain(
        list(range(Y)), list(range(X)), lambda i: i < x, recv_f, rows_f, back_f, state_f, 0
    )
    first += to_rows
    second += to_places
    loads[4].wait()
    loads[5].wait()
    for copy in first:
        copy.wait_send()

    for h in range(HEADS):
        lanes = slice(h * E, (h + 1) * E)
        g, inner = h // GROUP, slice(h % GROUP * PART, (h % GROUP + 1) * PART)
        if h % GROUP == 0:
            arrived_y(state_f.at[g], back_rsem.at[0, g], back_ssem.at[0, g])
        entering = state_f[g, :, inner].reshape(E, E).astype(BF16)
        half[h] = entering
        whole = att[:, lanes] + dot(qdec[:, lanes], entering, NN)
        att[:, lanes] = whole
        cotangent = gain[:, lanes] * grad[:, lanes].astype(F32)
        square, cross = whole * whole, cotangent * whole
        squares[...] = square if h == 0 else squares[...] + square
        crosses[...] = cross if h == 0 else crosses[...] + cross

    own = jnp.concatenate(
        [
            jnp.sum(jnp.transpose(squares[...]), axis=0, keepdims=True),
            jnp.sum(jnp.transpose(crosses[...]), axis=0, keepdims=True),
        ],
        axis=0,
    )
    pair[0] = own
    second.append(remote(pair.at[0], pair.at[1], pair_sem.at[0], pair_sem.at[1], ctx, other))
    second[-1].start()
    second[-1].wait_recv()
    stats[z] = own + pair[1]
    for step in Z_STEPS:
        to = along_z(step)
        second.append(
            remote(
                stats.at[z], stats.at[z], stat_ssem.at[to], stat_rsem.at[z], ctx, to * 2 + core
            )
        )
        second[-1].start()
    for step in Z_STEPS:
        at = along_z(step)
        remote(
            stats.at[at], stats.at[at], stat_ssem.at[at], stat_rsem.at[at], ctx, at * 2 + core
        ).wait_recv()
    sums = stats[0]
    for i in range(1, Z):
        sums = sums + stats[i]
    inverse_row = lax.rsqrt(sums[0:1] / (ATTENTION_HEADS * E) + EPSILON)
    slope_row = inverse_row * inverse_row * inverse_row * sums[1:2] / (ATTENTION_HEADS * E)
    squares[...] = columns(inverse_row)
    crosses[...] = columns(slope_row)

    for h in range(HEADS):
        lanes = slice(h * E, (h + 1) * E)
        inverse = squares[...]
        whole = att[:, lanes]
        scale = gain[:, lanes]
        here = (
            inverse * (scale * grad[:, lanes].astype(F32)) - whole * crosses[...]
        ).astype(BF16)
        datt[:, lanes] = here
        g, inner = h // GROUP, slice(h % GROUP * PART, (h % GROUP + 1) * PART)
        part_b[g, :, inner] = dot(qdec[:, lanes], here, TN).reshape(Y, PART, E)
        if h % GROUP == GROUP - 1:
            third += spread_y(
                lambda to: part_b.at[g, to], recv_b.at[g], part_ssem.at[1, g], part_rsem.at[1, g]
            )
            recv_b[g, y] = part_b[g, y]

    def backward(h, carry):
        lanes = pl.ds(pl.multiple_of(h * E, E), E)
        normed[:, lanes] = (gain[:, lanes] * att[:, lanes] * squares[...]).astype(BF16)
        entering = half[h]
        for r in range(BLOCK // TILE):
            rows, width = slice(r * TILE, (r + 1) * TILE), (r + 1) * TILE
            here = datt[rows, lanes]
            dprob = dot(here, v[:width, lanes], NT)
            dscore = (dprob * weights[h, rows, :width]).astype(BF16)
            dscores[h, rows, :width] = dscore
            gq[rows, lanes] = (
                dot(dscore, k[:width, lanes], NN) + rise[h, rows, :] * dot(here, entering, NT)
            ).astype(BF16)
        for c in range(BLOCK // TILE):
            place, later = slice(c * TILE, (c + 1) * TILE), slice(c * TILE, BLOCK)
            gk_part[place, lanes] = dot(dscores[h, later, place], q[later, lanes], TN)
            gv_part[place, lanes] = dot(probs[h, later, place], datt[later, lanes], TN)
        return carry

    lax.fori_loop(0, HEADS, backward, 0)
    to_rows, to_places = chain(
        list(reversed(range(Y))), list(reversed(range(X))), lambda i: i > x,
        recv_b, rows_b, back_b, state_b, 1,
    )
    third += to_rows
    fourth += to_places
    for copy in second + third:
        copy.wait_send()
    for h in range(HEADS):
        lanes = slice(h * E, (h + 1) * E)
        g, inner = h // GROUP, slice(h % GROUP * PART, (h % GROUP + 1) * PART)
        if h == HEADS - GROUP:
            for copy in fourth:
                copy.wait_send()
        if h % GROUP == 0:
            arrived_y(state_b.at[g], back_rsem.at[1, g], back_ssem.at[1, g])
        leaving = state_b[g, :, inner].reshape(E, E).astype(BF16)
        gk[:, lanes] = (
            gk_part[:, lanes] + fall[h] * dot(v[:, lanes], leaving, NT)
        ).astype(BF16)
        gv[:, lanes] = (gv_part[:, lanes] + dot(kdec[:, lanes], leaving, NN)).astype(BF16)


def write(*refs):
    sources, results, sem = refs[:4], refs[4:8], refs[8]
    stores = [
        pltpu.make_async_copy(src, dst, sem.at[n])
        for n, (src, dst) in enumerate(zip(sources, results))
    ]
    for store in stores:
        store.start()
    for store in stores:
        store.wait()


def per_device(queries, keys, values, log_decay, gain, grad_out):
    tile = jax.ShapeDtypeStruct((BLOCK, HEADS * E), BF16)
    flat16 = pltpu.VMEM((BLOCK, HEADS * E), BF16)
    flat32 = pltpu.VMEM((BLOCK, HEADS * E), F32)
    head32 = pltpu.VMEM((HEADS, BLOCK, E), F32)
    one32 = pltpu.VMEM((BLOCK, E), F32)
    square = (HEADS, BLOCK, BLOCK)
    parts = pltpu.VMEM((CHUNKS, Y, GROUP * PART, E), F32)
    across = pltpu.VMEM((CHUNKS, X, GROUP * PART, E), F32)
    sem = pltpu.SemaphoreType.DMA
    chain = [parts, parts, across, parts, parts]
    anywhere = pl.BlockSpec(memory_space=pl.ANY)
    vmem = pl.BlockSpec(memory_space=pltpu.VMEM)
    results = pl.pallas_call(
        kernel,
        out_shape=(pltpu.VMEM((BLOCK, HEADS * E), BF16),) * 4,
        in_specs=[anywhere] * 6,
        out_specs=(vmem,) * 4,
        scratch_shapes=[
            flat16, flat16, flat16,
            pltpu.VMEM((HEADS, BLOCK), F32), pltpu.VMEM((1, HEADS * E), F32), flat16,
            pltpu.VMEM((HEADS, BLOCK), F32), head32, head32, head32, flat16, flat16,
            pltpu.VMEM(square, F32), pltpu.VMEM(square, BF16), pltpu.VMEM(square, BF16),
            flat32, one32, one32, flat16, pltpu.VMEM((HEADS, E, E), BF16), flat32, flat32,
            pltpu.VMEM((HEADS, 1, TILE), F32), pltpu.VMEM((Y, HEADS, 1, TILE), F32),
            pltpu.VMEM((X, HEADS, 1, TILE), F32),
            *chain, *chain,
            pltpu.VMEM((2, 2, BLOCK), F32), pltpu.VMEM((Z, 2, BLOCK), F32),
            sem((6,)),
            sem((Y,)), sem((Y,)), sem((X,)), sem((X,)),
            *[sem((2, CHUNKS, n)) for n in (Y, Y, X, X, Y, Y)],
            sem((2,)), sem((Z,)), sem((Z,)),
        ],
        compiler_params=pltpu.CompilerParams(
            collective_id=0,
            has_side_effects=True,
            vmem_limit_bytes=67043328 - 4 * BLOCK * HEADS * E * 2,
        ),
        name="layer",
    )(queries, keys, values, log_decay, gain.reshape(1, -1), grad_out)
    return pl.pallas_call(
        write,
        out_shape=(tile,) * 4,
        in_specs=[vmem] * 4,
        out_specs=(anywhere,) * 4,
        scratch_shapes=[sem((4,))],
        compiler_params=pltpu.CompilerParams(vmem_limit_bytes=16 * 2**20),
        name="write",
    )(*results)


def solution(mesh):
    in_specs = (
        P("ctx", "tp"),
        P("ctx", "tp"),
        P("ctx", "tp"),
        P("tp", "ctx"),
        P("tp"),
        P("ctx", "tp"),
    )
    out_specs = (P("ctx", "tp"), P("ctx", "tp"), P("ctx", "tp"), P("ctx", "tp"))
    return jax.shard_map(
        per_device, mesh=mesh, in_specs=in_specs, out_specs=out_specs, check_vma=False
    )
```

```python
import jax
import jax.numpy as jnp
from jax import lax
from jax.experimental import pallas as pl
from jax.experimental.pallas import tpu as pltpu
from jax.sharding import PartitionSpec as P

ATTENTION_HEADS = 64
E = 128
BLOCK = 512
EPSILON = 1e-05

X, Y, Z, TP = 4, 8, 8, 16
HEADS = ATTENTION_HEADS // TP
PART = E // Y
GROUP = 2
CHUNKS = HEADS // GROUP
LAG = 1
TILE = 128
F32, BF16 = jnp.float32, jnp.bfloat16

NN = (((1,), (0,)), ((), ()))
NT = (((1,), (1,)), ((), ()))
TN = (((0,), (0,)), ((), ()))


def dot(a, b, dims):
    return lax.dot_general(a, b, dims, preferred_element_type=F32)


def columns(row, width=TILE):
    return jnp.transpose(jnp.broadcast_to(row, (width, row.shape[1])))


def kernel(
    q_in, k_in, v_in, decay_in, gain_in, grad_in,
    normed, gq, gk, gv,
    q, k, v, decay, gain, grad,
    cum, rise, fall, qdec, kdec, weights, probs, dscores,
    att, squares, crosses, datt, half, gk_part, gv_part,
    factor_send, factor_recv, row_factor,
    part_f, recv_f, rows_f, back_f, state_f,
    part_b, recv_b, rows_b, back_b, state_b,
    pair, stats,
    load_sem,
    factor_ssem, factor_rsem, row_ssem, row_rsem,
    part_ssem, part_rsem, rows_ssem, rows_rsem, back_ssem, back_rsem,
    pair_sem, stat_ssem, stat_rsem,
):
    ctx, tp = lax.axis_index("ctx"), lax.axis_index("tp")
    x, y = ctx // Y, ctx % Y
    z, core = tp // 2, tp % 2
    other = z * 2 + 1 - core

    loads = [
        pltpu.make_async_copy(src, dst, load_sem.at[n])
        for n, (src, dst) in enumerate(
            ((decay_in, decay), (k_in, k), (v_in, v), (q_in, q), (gain_in, gain), (grad_in, grad))
        )
    ]
    for load in loads:
        load.start()

    def along_y(step):
        return (y + step) % Y

    def along_x(step):
        return (x + step) % X

    def along_z(step):
        return (z + step) % Z

    Y_STEPS = (4, 3, 5, 2, 6, 1, 7)
    X_STEPS = (2, 1, 3)
    Z_STEPS = (4, 3, 5, 2, 6, 1, 7)

    barrier = pltpu.get_barrier_semaphore()
    for step in Y_STEPS:
        pl.semaphore_signal(
            barrier, 1, device_id=(x * Y + along_y(step), tp), device_id_type=pl.DeviceIdType.MESH
        )
    for step in X_STEPS:
        pl.semaphore_signal(
            barrier, 1, device_id=(along_x(step) * Y + y, tp), device_id_type=pl.DeviceIdType.MESH
        )
    for step in Z_STEPS:
        pl.semaphore_signal(
            barrier, 1, device_id=(ctx, along_z(step) * 2 + core), device_id_type=pl.DeviceIdType.MESH
        )
    pl.semaphore_signal(barrier, 1, device_id=(ctx, other), device_id_type=pl.DeviceIdType.MESH)

    def remote(src, dst, ssem, rsem, to_ctx, to_tp):
        return pltpu.make_async_remote_copy(
            src_ref=src, dst_ref=dst, send_sem=ssem, recv_sem=rsem,
            device_id=(to_ctx, to_tp), device_id_type=pl.DeviceIdType.MESH,
        )

    def spread_y(source, target, ssem, rsem):
        copies = []
        for step in Y_STEPS:
            to = along_y(step)
            copies.append(
                remote(source(to), target.at[y], ssem.at[to], rsem.at[y], x * Y + to, tp)
            )
            copies[-1].start()
        return copies

    def spread_x(source, target, ssem, rsem):
        copies = []
        for step in X_STEPS:
            to = along_x(step)
            copies.append(
                remote(source, target.at[x], ssem.at[to], rsem.at[x], to * Y + y, tp)
            )
            copies[-1].start()
        return copies

    def arrived_y(target, rsem, ssem):
        for step in Y_STEPS:
            at = along_y(step)
            remote(target.at[at], target.at[at], ssem.at[at], rsem.at[at], x * Y + at, tp).wait_recv()

    def arrived_x(target, rsem, ssem):
        for step in X_STEPS:
            at = along_x(step)
            remote(target.at[at], target.at[at], ssem.at[at], rsem.at[at], at * Y + y, tp).wait_recv()

    first, second, third, fourth = [], [], [], []

    loads[0].wait()
    tokens = lax.broadcasted_iota(jnp.int32, (TILE, TILE), 0)
    until = lax.broadcasted_iota(jnp.int32, (TILE, TILE), 1)
    upper = jnp.where(tokens <= until, 1.0, 0.0).astype(F32)
    before = jnp.zeros((HEADS, 1), F32)
    for c in range(BLOCK // TILE):
        place = slice(c * TILE, (c + 1) * TILE)
        summed = before + lax.dot_general(
            decay[:, place], upper, NN, precision=lax.Precision.HIGHEST,
            preferred_element_type=F32,
        )
        cum[:, place] = summed
        before = summed[:, TILE - 1 : TILE]
    for h in range(HEADS):
        total = cum[h : h + 1, BLOCK - 1 : BLOCK]
        factor_send[h] = jnp.exp(jnp.broadcast_to(total, (1, TILE)))
    loads[1].wait()
    loads[2].wait()
    for h in range(HEADS):
        lanes = slice(h * E, (h + 1) * E)
        row = cum[h : h + 1, :]
        drop = columns(jnp.exp(row[:, BLOCK - 1 : BLOCK] - row))
        fall[h] = drop
        kdec[:, lanes] = (k[:, lanes].astype(F32) * drop).astype(BF16)
        g, inner = h // GROUP, slice(h % GROUP * PART, (h % GROUP + 1) * PART)
        part_f[g, :, inner] = dot(kdec[:, lanes], v[:, lanes], TN).reshape(Y, PART, E)
        if h == 0:
            pl.semaphore_wait(barrier, Y + X + Z - 2)
            first += spread_y(lambda to: factor_send, factor_recv, factor_ssem, factor_rsem)
            factor_recv[y] = factor_send[...]
        if h % GROUP == GROUP - 1:
            first += spread_y(
                lambda to: part_f.at[g, to], recv_f.at[g], part_ssem.at[0, g], part_rsem.at[0, g]
            )
            recv_f[g, y] = part_f[g, y]

    loads[3].wait()

    def inside(h, carry):
        lanes = pl.ds(pl.multiple_of(h * E, E), E)
        row = cum[pl.ds(h, 1), :]
        wide = columns(row)
        grow = jnp.exp(wide)
        rise[h] = grow
        qdec[:, lanes] = (q[:, lanes].astype(F32) * grow).astype(BF16)
        for r in range(BLOCK // TILE):
            rows, width = slice(r * TILE, (r + 1) * TILE), (r + 1) * TILE
            scores = dot(q[rows, lanes], k[:width, lanes], NT)
            mine = wide[rows]
            pieces = []
            for c in range(r + 1):
                spread = mine - row[:, c * TILE : (c + 1) * TILE]
                if c == r:
                    down = lax.broadcasted_iota(jnp.int32, (TILE, TILE), 0)
                    across = lax.broadcasted_iota(jnp.int32, (TILE, TILE), 1)
                    spread = jnp.where(down >= across, spread, -1e30)
                pieces.append(jnp.exp(spread))
            weight = pieces[0] if r == 0 else jnp.concatenate(pieces, axis=1)
            weights[h, rows, :width] = weight
            prob = (scores * weight).astype(BF16)
            probs[h, rows, :width] = prob
            att[rows, lanes] = dot(prob, v[:width, lanes], NN)
        return carry

    lax.fori_loop(0, HEADS, inside, 0)

    arrived_y(factor_recv, factor_rsem, factor_ssem)
    product = factor_recv[0]
    for j in range(1, Y):
        product = product * factor_recv[j]
    row_factor[x] = product
    first += spread_x(row_factor.at[x], row_factor, row_ssem, row_rsem)

    def chain(order_y, order_x, before, recv, rows, back, state, n):
        to_rows, to_places = [], []
        inners = [slice(i * PART, (i + 1) * PART) for i in range(GROUP)]
        for turn in range(CHUNKS + LAG):
            g = turn
            if g < CHUNKS:
                arrived_y(recv.at[g], part_rsem.at[n, g], part_ssem.at[n, g])
                for i, inner in enumerate(inners):
                    h = g * GROUP + i
                    running = recv[g, order_y[0], inner]
                    back[g, order_y[0], inner] = jnp.zeros((PART, E), F32)
                    for j in order_y[1:]:
                        back[g, j, inner] = running
                        running = factor_recv[j, h] * running + recv[g, j, inner]
                    rows[g, x, inner] = running
                to_rows += spread_x(
                    rows.at[g, x], rows.at[g], rows_ssem.at[n, g], rows_rsem.at[n, g]
                )
            if n == 0 and turn == LAG:
                arrived_x(row_factor, row_rsem, row_ssem)
            g = turn - LAG
            if g >= 0:
                arrived_x(rows.at[g], rows_rsem.at[n, g], rows_ssem.at[n, g])
                for i, inner in enumerate(inners):
                    h = g * GROUP + i
                    enter = jnp.zeros((PART, E), F32)
                    for k in order_x[:-1]:
                        enter = jnp.where(
                            before(k), row_factor[k, h] * enter + rows[g, k, inner], enter
                        )
                    for j in order_y:
                        back[g, j, inner] = back[g, j, inner] + enter
                        enter = factor_recv[j, h] * enter
                to_places += spread_y(
                    lambda to: back.at[g, to], state.at[g], back_ssem.at[n, g], back_rsem.at[n, g]
                )
                state[g, y] = back[g, y]
        return to_rows, to_places

    to_rows, to_places = chain(
        list(range(Y)), list(range(X)), lambda i: i < x, recv_f, rows_f, back_f, state_f, 0
    )
    first += to_rows
    second += to_places
    loads[4].wait()
    loads[5].wait()
    for copy in first:
        copy.wait_send()

    for h in range(HEADS):
        lanes = slice(h * E, (h + 1) * E)
        g, inner = h // GROUP, slice(h % GROUP * PART, (h % GROUP + 1) * PART)
        if h % GROUP == 0:
            arrived_y(state_f.at[g], back_rsem.at[0, g], back_ssem.at[0, g])
        entering = state_f[g, :, inner].reshape(E, E).astype(BF16)
        half[h] = entering
        whole = att[:, lanes] + dot(qdec[:, lanes], entering, NN)
        att[:, lanes] = whole
        cotangent = gain[:, lanes] * grad[:, lanes].astype(F32)
        square, cross = whole * whole, cotangent * whole
        squares[...] = square if h == 0 else squares[...] + square
        crosses[...] = cross if h == 0 else crosses[...] + cross

    own = jnp.concatenate(
        [
            jnp.sum(jnp.transpose(squares[...]), axis=0, keepdims=True),
            jnp.sum(jnp.transpose(crosses[...]), axis=0, keepdims=True),
        ],
        axis=0,
    )
    pair[0] = own
    second.append(remote(pair.at[0], pair.at[1], pair_sem.at[0], pair_sem.at[1], ctx, other))
    second[-1].start()
    second[-1].wait_recv()
    stats[z] = own + pair[1]
    for step in Z_STEPS:
        to = along_z(step)
        second.append(
            remote(
                stats.at[z], stats.at[z], stat_ssem.at[to], stat_rsem.at[z], ctx, to * 2 + core
            )
        )
        second[-1].start()
    for step in Z_STEPS:
        at = along_z(step)
        remote(
            stats.at[at], stats.at[at], stat_ssem.at[at], stat_rsem.at[at], ctx, at * 2 + core
        ).wait_recv()
    sums = stats[0]
    for i in range(1, Z):
        sums = sums + stats[i]
    inverse_row = lax.rsqrt(sums[0:1] / (ATTENTION_HEADS * E) + EPSILON)
    slope_row = inverse_row * inverse_row * inverse_row * sums[1:2] / (ATTENTION_HEADS * E)
    squares[...] = columns(inverse_row)
    crosses[...] = columns(slope_row)

    for h in range(HEADS):
        lanes = slice(h * E, (h + 1) * E)
        inverse = squares[...]
        whole = att[:, lanes]
        scale = gain[:, lanes]
        here = (
            inverse * (scale * grad[:, lanes].astype(F32)) - whole * crosses[...]
        ).astype(BF16)
        datt[:, lanes] = here
        g, inner = h // GROUP, slice(h % GROUP * PART, (h % GROUP + 1) * PART)
        part_b[g, :, inner] = dot(qdec[:, lanes], here, TN).reshape(Y, PART, E)
        if h % GROUP == GROUP - 1:
            third += spread_y(
                lambda to: part_b.at[g, to], recv_b.at[g], part_ssem.at[1, g], part_rsem.at[1, g]
            )
            recv_b[g, y] = part_b[g, y]

    def backward(h, carry):
        lanes = pl.ds(pl.multiple_of(h * E, E), E)
        normed[:, lanes] = (gain[:, lanes] * att[:, lanes] * squares[...]).astype(BF16)
        entering = half[h]
        for r in range(BLOCK // TILE):
            rows, width = slice(r * TILE, (r + 1) * TILE), (r + 1) * TILE
            here = datt[rows, lanes]
            dprob = dot(here, v[:width, lanes], NT)
            dscore = (dprob * weights[h, rows, :width]).astype(BF16)
            dscores[h, rows, :width] = dscore
            gq[rows, lanes] = (
                dot(dscore, k[:width, lanes], NN) + rise[h, rows, :] * dot(here, entering, NT)
            ).astype(BF16)
        for c in range(BLOCK // TILE):
            place, later = slice(c * TILE, (c + 1) * TILE), slice(c * TILE, BLOCK)
            gk_part[place, lanes] = dot(dscores[h, later, place], q[later, lanes], TN)
            gv_part[place, lanes] = dot(probs[h, later, place], datt[later, lanes], TN)
        return carry

    lax.fori_loop(0, HEADS, backward, 0)
    to_rows, to_places = chain(
        list(reversed(range(Y))), list(reversed(range(X))), lambda i: i > x,
        recv_b, rows_b, back_b, state_b, 1,
    )
    third += to_rows
    fourth += to_places
    for copy in second + third:
        copy.wait_send()
    for h in range(HEADS):
        lanes = slice(h * E, (h + 1) * E)
        g, inner = h // GROUP, slice(h % GROUP * PART, (h % GROUP + 1) * PART)
        if h == HEADS - GROUP:
            for copy in fourth:
                copy.wait_send()
        if h % GROUP == 0:
            arrived_y(state_b.at[g], back_rsem.at[1, g], back_ssem.at[1, g])
        leaving = state_b[g, :, inner].reshape(E, E).astype(BF16)
        gk[:, lanes] = (
            gk_part[:, lanes] + fall[h] * dot(v[:, lanes], leaving, NT)
        ).astype(BF16)
        gv[:, lanes] = (gv_part[:, lanes] + dot(kdec[:, lanes], leaving, NN)).astype(BF16)


def write(*refs):
    sources, results, sem = refs[:4], refs[4:8], refs[8]
    stores = [
        pltpu.make_async_copy(src, dst, sem.at[n])
        for n, (src, dst) in enumerate(zip(sources, results))
    ]
    for store in stores:
        store.start()
    for store in stores:
        store.wait()


def per_device(queries, keys, values, log_decay, gain, grad_out):
    tile = jax.ShapeDtypeStruct((BLOCK, HEADS * E), BF16)
    flat16 = pltpu.VMEM((BLOCK, HEADS * E), BF16)
    flat32 = pltpu.VMEM((BLOCK, HEADS * E), F32)
    head32 = pltpu.VMEM((HEADS, BLOCK, E), F32)
    one32 = pltpu.VMEM((BLOCK, E), F32)
    square = (HEADS, BLOCK, BLOCK)
    parts = pltpu.VMEM((CHUNKS, Y, GROUP * PART, E), F32)
    across = pltpu.VMEM((CHUNKS, X, GROUP * PART, E), F32)
    sem = pltpu.SemaphoreType.DMA
    chain = [parts, parts, across, parts, parts]
    anywhere = pl.BlockSpec(memory_space=pl.ANY)
    vmem = pl.BlockSpec(memory_space=pltpu.VMEM)
    results = pl.pallas_call(
        kernel,
        out_shape=(pltpu.VMEM((BLOCK, HEADS * E), BF16),) * 4,
        in_specs=[anywhere] * 6,
        out_specs=(vmem,) * 4,
        scratch_shapes=[
            flat16, flat16, flat16,
            pltpu.VMEM((HEADS, BLOCK), F32), pltpu.VMEM((1, HEADS * E), F32), flat16,
            pltpu.VMEM((HEADS, BLOCK), F32), head32, head32, flat16, flat16,
            pltpu.VMEM(square, F32), pltpu.VMEM(square, BF16), pltpu.VMEM(square, BF16),
            flat32, one32, one32, flat16, pltpu.VMEM((HEADS, E, E), BF16), flat32, flat32,
            pltpu.VMEM((HEADS, 1, TILE), F32), pltpu.VMEM((Y, HEADS, 1, TILE), F32),
            pltpu.VMEM((X, HEADS, 1, TILE), F32),
            *chain, *chain,
            pltpu.VMEM((2, 2, BLOCK), F32), pltpu.VMEM((Z, 2, BLOCK), F32),
            sem((6,)),
            sem((Y,)), sem((Y,)), sem((X,)), sem((X,)),
            *[sem((2, CHUNKS, n)) for n in (Y, Y, X, X, Y, Y)],
            sem((2,)), sem((Z,)), sem((Z,)),
        ],
        compiler_params=pltpu.CompilerParams(
            collective_id=0,
            has_side_effects=True,
            vmem_limit_bytes=67043328 - 4 * BLOCK * HEADS * E * 2,
        ),
        name="layer",
    )(queries, keys, values, log_decay, gain.reshape(1, -1), grad_out)
    return pl.pallas_call(
        write,
        out_shape=(tile,) * 4,
        in_specs=[vmem] * 4,
        out_specs=(anywhere,) * 4,
        scratch_shapes=[sem((4,))],
        compiler_params=pltpu.CompilerParams(vmem_limit_bytes=16 * 2**20),
        name="write",
    )(*results)


def solution(mesh):
    in_specs = (
        P("ctx", "tp"),
        P("ctx", "tp"),
        P("ctx", "tp"),
        P("tp", "ctx"),
        P("tp"),
        P("ctx", "tp"),
    )
    out_specs = (P("ctx", "tp"), P("ctx", "tp"), P("ctx", "tp"), P("ctx", "tp"))
    return jax.shard_map(
        per_device, mesh=mesh, in_specs=in_specs, out_specs=out_specs, check_vma=False
    )
```
